128 devices in a mesh: view: 8 (over y, z_lo), depth: 16 (over x, z_hi, core).
Axes of the slice: x: 4, y: 4, z: 4 (z_hi: 2, z_lo: 2; z = z_hi * 2 + z_lo), core: 2. Of those that a mesh axis runs over, the one named last changes fastest.
Arguments:
- estimate: float32 [128, 128, 256], P('depth', 'view'), may hold values from 0.5 to 2
- observed: float32 [16, 128, 128, 256], P('view', 'depth'), may hold values from 0.05 to 30, as said below
- voxel_weights: bfloat16 [16, 8, 128, 128, 256], P('view', None, 'depth'), may hold values from 0.029907227 to 0.29882812
- lateral_taps: float32 [16, 8, 2, 9], P('view'), may hold values from 0.05 to 1
- axial_taps: float32 [16, 9], P('view'), may hold values from 0.05 to 1
Outputs:
- updated: float32 [128, 128, 256], P('depth', 'view')
- divergence: float32 [16], P('view')
The draws below stay inside these ranges and needn't reach their ends.
Inputs may be any that keep to these rules, and one draw needn't show every extreme that they name: `observed`: strictly positive.
All inputs are finite; a program needn't handle non-finite values.
Results may differ from the reference program's by a relative error of at most 0.0003.
Values sent between devices are 32-bit elements; how exact they have to be, the bound alone decides.
A program may use at most 128 MiB of HBM per device.

```python
import math
import jax
import jax.numpy as jnp
from jax import lax

BASES = 8
TAPS = 9
RADIUS = 4
ITERS = 2
NY = 128
NX = 256
VIEWS = 16
NZ = 128


def draw_observed(key, part):
    key_values, key_facing = jax.random.split(key, 2)
    volume_shape = (VIEWS, NZ, NY, NX)
    facing = jnp.where(jax.random.bernoulli(key_facing, 0.5, (VIEWS,)), 1.0, -1.0).astype(jnp.float32)
    depth_frac = jnp.arange(NZ, dtype=jnp.float32) / max(NZ - 1, 1) - 0.5
    intensity = jnp.exp(jax.random.uniform(key_values, volume_shape, jnp.float32, jnp.log(0.1), jnp.log(10.0)))
    strength = jnp.log(3.0)
    profile = jnp.exp(strength * facing[:, None] * depth_frac[None, :])
    return intensity * profile[:, :, None, None]


def steps_of(own_key, dims, cuts, low, high):
    factor_of, own = 1.0, jax.random.fold_in(own_key, 6)
    for axis_at, shards_of in cuts:
        draws = jnp.exp(jax.random.uniform(jax.random.fold_in(own, axis_at), (shards_of,), jnp.float32, low / len(cuts), high / len(cuts)))
        factor_of = factor_of * jnp.repeat(draws, dims[axis_at] // shards_of).reshape([-1 if axis == axis_at else 1 for axis in range(len(dims))])
    return factor_of


def setup_inputs(seed: int = 0) -> dict:
    key_of = jax.random.split(jax.random.key(seed), 6)
    return {
        "estimate": jnp.clip(jnp.exp(math.log(2.0) - 1.3862944 * jax.random.uniform(key_of[0], (NZ, NY, NX), jnp.float32) ** steps_of(key_of[0], (NZ, NY, NX), ((0, 16), (1, 8)), -0.2, 0.2)), 0.5, 2.0),
        "observed": draw_observed(jax.random.fold_in(key_of[5], 71), 0),
        "voxel_weights": jnp.clip(jnp.exp(math.log(0.29882812) - 2.30176843 * jax.random.uniform(key_of[2], (VIEWS, BASES, NZ, NY, NX), jnp.float32) ** steps_of(key_of[2], (VIEWS, BASES, NZ, NY, NX), ((0, 8), (2, 16)), -0.2, 0.2)), 0.029907227, 0.29882812).astype(jnp.bfloat16),
        "lateral_taps": jnp.clip(jnp.exp(math.log(1.0) - 2.9957323 * jax.random.uniform(key_of[3], (VIEWS, BASES, 2, TAPS), jnp.float32) ** steps_of(key_of[3], (VIEWS, BASES, 2, TAPS), ((0, 8),), -0.2, 0.2)), 0.05, 1.0),
        "axial_taps": jnp.clip(jnp.exp(math.log(1.0) - 2.9957323 * jax.random.uniform(key_of[4], (VIEWS, TAPS), jnp.float32) ** steps_of(key_of[4], (VIEWS, TAPS), ((0, 8),), -0.2, 0.2)), 0.05, 1.0),
    }


def depth_forward(volume, depth_taps):
    planes = volume.shape[0]
    padded = jnp.pad(volume, ((RADIUS, RADIUS), (0, 0), (0, 0)))
    summed = jnp.zeros(volume.shape, jnp.float32)
    for tap_index in range(TAPS):
        summed = summed + depth_taps[tap_index] * padded[tap_index:tap_index + planes]
    return summed


def depth_adjoint(volume, depth_taps):
    planes = volume.shape[0]
    padded = jnp.pad(volume, ((RADIUS, RADIUS), (0, 0), (0, 0)))
    summed = jnp.zeros(volume.shape, jnp.float32)
    for tap_index in range(TAPS):
        offset = 2 * RADIUS - tap_index
        summed = summed + depth_taps[tap_index] * padded[offset:offset + planes]
    return summed


def lateral_forward(volume, weights, lateral):
    height = volume.shape[1]
    breadth = volume.shape[2]
    padded = jnp.pad(volume, ((0, 0), (RADIUS, RADIUS), (0, 0)))
    stacked = jnp.zeros((BASES,) + volume.shape, jnp.float32)
    for tap_index in range(TAPS):
        stacked = stacked + lateral[:, 0, tap_index].reshape(-1, 1, 1, 1) * padded[None, :, tap_index:tap_index + height, :]
    padded = jnp.pad(stacked, ((0, 0), (0, 0), (0, 0), (RADIUS, RADIUS)))
    blurred = jnp.zeros(stacked.shape, jnp.float32)
    for tap_index in range(TAPS):
        blurred = blurred + lateral[:, 1, tap_index].reshape(-1, 1, 1, 1) * padded[:, :, :, tap_index:tap_index + breadth]
    return jnp.sum(weights.astype(jnp.float32) * blurred, axis=0)


def lateral_adjoint(values, weights, lateral):
    height = values.shape[1]
    breadth = values.shape[2]
    stacked = weights.astype(jnp.float32) * values[None]
    padded = jnp.pad(stacked, ((0, 0), (0, 0), (0, 0), (RADIUS, RADIUS)))
    blurred = jnp.zeros(stacked.shape, jnp.float32)
    for tap_index in range(TAPS):
        offset = 2 * RADIUS - tap_index
        blurred = blurred + lateral[:, 1, tap_index].reshape(-1, 1, 1, 1) * padded[:, :, :, offset:offset + breadth]
    padded = jnp.pad(blurred, ((0, 0), (0, 0), (RADIUS, RADIUS), (0, 0)))
    summed = jnp.zeros(stacked.shape, jnp.float32)
    for tap_index in range(TAPS):
        offset = 2 * RADIUS - tap_index
        summed = summed + lateral[:, 0, tap_index].reshape(-1, 1, 1, 1) * padded[:, :, offset:offset + height, :]
    return jnp.sum(summed, axis=0)


def reference(estimate, observed, voxel_weights, lateral_taps, axial_taps):
    lateral_all = lateral_taps / jnp.sum(lateral_taps, axis=-1, keepdims=True)
    axial_all = axial_taps / jnp.sum(axial_taps, axis=-1, keepdims=True)
    voxel_total = estimate.shape[0] * estimate.shape[1] * estimate.shape[2]

    def sensitivity_of(member):
        weights, lateral, depth_taps = member
        unity = jnp.ones(estimate.shape, jnp.float32)
        return depth_adjoint(lateral_adjoint(unity, weights, lateral), depth_taps)

    sensitivity = lax.map(sensitivity_of, (voxel_weights, lateral_all, axial_all))
    current = estimate
    divergence = jnp.zeros((VIEWS,), jnp.float32)
    for iteration in range(ITERS):
        def view_step(log_total, member):
            counts, weights, lateral, depth_taps, sens_view = member
            predicted = lateral_forward(depth_forward(current, depth_taps), weights, lateral)
            ratios = counts / predicted
            projected = depth_adjoint(lateral_adjoint(ratios, weights, lateral), depth_taps)
            fidelity = jnp.sum(counts * jnp.log(ratios) - counts + predicted) / voxel_total
            return log_total + jnp.log(projected / sens_view), fidelity

        log_total, divergence = lax.scan(view_step, jnp.zeros(estimate.shape, jnp.float32), (observed, voxel_weights, lateral_all, axial_all, sensitivity))
        current = current * jnp.exp(log_total / VIEWS)
    return current, divergence
```

```python
import numpy as np
import jax
import jax.numpy as jnp
from jax import lax
from jax.experimental import pallas as pl
from jax.experimental.pallas import tpu as pltpu
from jax.sharding import PartitionSpec as P

BASES = 8
TAPS = 9
RADIUS = 4
ITERS = 2
F32 = jnp.float32
BF16 = jnp.bfloat16
ROWS = 16
CHUNK = 32


def spread(count, stride, reach):
    return 1.0 + reach * np.mod(stride * np.arange(count) + 0.13, 1.0)


def scale_tiles():
    rows = np.broadcast_to(spread(8, 0.5698402910, 0.37)[:, None], (8, 256))
    lanes = np.broadcast_to(spread(256, 0.7548776662, 0.41)[None, :], (8, 256))
    return np.stack([rows, 1.0 / rows, lanes, 1.0 / lanes, lanes / rows]).astype(np.float32)


def kernel(
    est, obs, wgt, base_x, base_y, scale, axial, step, tiles,
    out, div_out,
    w, ob, tyf, tya, txf, txa, g, mid, field, s_field, r_field, acc, ratio, log_s, log_r, far, near,
    zbuf, sums, peers,
    load_sem, ag_send, ag_recv, halo_send, halo_recv, rs_send, rs_recv, div_send, div_recv,
):
    vi = lax.axis_index("view")
    d = lax.axis_index("depth")
    y = vi // 2
    zl = vi % 2
    core = d % 2
    v_up = ((y + 1) % 4) * 2 + zl
    v_dn = ((y + 3) % 4) * 2 + zl
    v_z = vi + 1 - 2 * zl
    d_up = (d + 1) % 16
    d_dn = (d + 15) % 16
    d_out = (d + 15 + 2 * core) % 16
    d_in = d + 1 - 2 * core
    partners = [d + 1 - 2 * (d % 2), d + 2 - 4 * ((d // 2) % 2), d + 4 - 8 * ((d // 4) % 2), d + 8 - 16 * (d // 8)]

    loads = [
        pltpu.make_async_copy(est, field.at[pl.ds(4, 8), pl.ds(pl.multiple_of(vi * ROWS, ROWS), ROWS)], load_sem.at[0]),
        pltpu.make_async_copy(wgt.at[0], w.at[0], load_sem.at[1]),
        pltpu.make_async_copy(wgt.at[1], w.at[1], load_sem.at[2]),
        pltpu.make_async_copy(obs, ob, load_sem.at[3]),
    ]
    for copy in loads:
        copy.start()

    barrier = pltpu.get_barrier_semaphore()
    greeted = [
        {"view": v_up}, {"view": v_dn}, {"view": v_z}, {"depth": d_up}, {"depth": d_dn},
        {"depth": partners[1]}, {"depth": partners[2]}, {"depth": partners[3]},
    ]
    for who in greeted:
        pl.semaphore_signal(barrier, inc=1, device_id=who, device_id_type=pl.DeviceIdType.MESH)
    pl.semaphore_wait(barrier, len(greeted))

    def remote(src, dst, send, recv, who):
        return pltpu.make_async_remote_copy(
            src_ref=src, dst_ref=dst, send_sem=send, recv_sem=recv,
            device_id=who, device_id_type=pl.DeviceIdType.MESH,
        )

    def block(first, count, owner):
        return field.at[pl.ds(first, count), pl.ds(pl.multiple_of(owner * ROWS, ROWS), ROWS)]

    def gather(it, part):
        first, count = ((4, 8), (12 * core, 4))[part]
        base = part * 7

        def hop(slot, owner, who):
            ref = block(first, count, owner)
            return remote(ref, ref, ag_send.at[it, base + slot], ag_recv.at[it, base + slot], who)

        mate = v_z
        return [
            hop(0, vi, {"view": v_z}),
            hop(1, vi, {"view": v_up}),
            hop(2, vi, {"view": v_dn}),
            hop(3, mate, {"view": v_up}),
            hop(4, mate, {"view": v_dn}),
            hop(5, v_dn, {"view": v_up}),
            hop(6, v_up + 1 - 2 * zl, {"view": v_dn}),
        ]

    def outer(it):
        return remote(
            block(4 + 4 * core, 4, vi), block(12 - 12 * core, 4, vi),
            ag_send.at[it, 14], ag_recv.at[it, 14], {"depth": d_out},
        )

    def inner(it):
        return remote(
            field.at[pl.ds(8 - 4 * core, 4)], field.at[pl.ds(12 * core, 4)],
            ag_send.at[it, 15], ag_recv.at[it, 15], {"depth": d_in},
        )

    def gather_first(it):
        outer(it).start()
        hops = gather(it, 0)
        for slot in (1, 2, 0):
            hops[slot].start()
        outer(it).wait_recv()
        hops = gather(it, 1)
        for slot in (1, 2, 0):
            hops[slot].start()

    def gather_second(it):
        for part in (0, 1):
            hops = gather(it, part)
            hops[0].wait_recv()
            hops[3].start()
            hops[4].start()
            hops[1].wait_recv()
            hops[5].start()

    def gather_third(it):
        for part in (0, 1):
            hops = gather(it, part)
            hops[4].wait_recv()
            hops[6].start()

    def gather_last(it):
        hops = gather(it, 0)
        for slot in (2, 3, 5, 6):
            hops[slot].wait_recv()
        inner(it).start()
        hops = gather(it, 1)
        for slot in (2, 3, 5, 6):
            hops[slot].wait_recv()
        inner(it).wait_recv()
        for part in (0, 1):
            for hop in gather(it, part):
                hop.wait_send()
        outer(it).wait_send()
        inner(it).wait_send()

        @pl.when(d == 0)
        def _():
            field[pl.ds(0, 4)] = jnp.zeros((4, 128, 256), F32)

        @pl.when(d == 15)
        def _():
            field[pl.ds(12, 4)] = jnp.zeros((4, 128, 256), F32)

    order = [(y + 2) % 4, (y + 1) % 4, (y + 3) % 4, y]

    def halo(buf, turn, v, c, up):
        rows = pl.ds(pl.multiple_of(order[c] * CHUNK, CHUNK), CHUNK)
        source, target = (8, 0) if up else (4, 12)
        slot = (v * 4 + c) * 2 + up
        return remote(
            buf.at[v, pl.ds(source, 4), rows], buf.at[v, pl.ds(target, 4), rows],
            halo_send.at[turn, slot], halo_recv.at[turn, slot], {"depth": d_up if up else d_dn},
        )

    def send_halos(buf, turn, v):
        for c in range(4):
            halo(buf, turn, v, c, 0).start()
            halo(buf, turn, v, c, 1).start()

    def wait_halo_chunk(buf, turn, c):
        for v in (0, 1):
            for up in (0, 1):
                halo(buf, turn, v, c, up).wait_recv()
        rows = pl.ds(pl.multiple_of(order[c] * CHUNK, CHUNK), CHUNK)

        @pl.when(d == 0)
        def _():
            buf[:, pl.ds(0, 4), rows] = jnp.zeros((2, 4, CHUNK, 256), F32)

        @pl.when(d == 15)
        def _():
            buf[:, pl.ds(12, 4), rows] = jnp.zeros((2, 4, CHUNK, 256), F32)

    def wait_halo_sends(buf, turn):
        for v in (0, 1):
            for c in range(4):
                for up in (0, 1):
                    halo(buf, turn, v, c, up).wait_send()

    def rs_hops(it):
        far_rows = order[0] * CHUNK
        up_rows = order[1] * CHUNK
        dn_rows = order[2] * CHUNK
        mate_rows = v_z * ROWS

        def cut(start, count):
            return log_r.at[:, pl.ds(pl.multiple_of(start, ROWS), count)]

        def hop(slot, src, dst, who):
            return remote(src, dst, rs_send.at[it, slot], rs_recv.at[it, slot], who)

        return [
            hop(0, cut(far_rows, ROWS), far.at[0], {"view": v_up}),
            hop(1, cut(far_rows + ROWS, ROWS), far.at[1], {"view": v_dn}),
            hop(2, cut(up_rows, CHUNK), near.at[0], {"view": v_up}),
            hop(3, cut(dn_rows, CHUNK), near.at[1], {"view": v_dn}),
            hop(4, cut(mate_rows, ROWS), zbuf, {"view": v_z}),
        ]

    def build(i, carry):
        v = i // 8
        b = i % 8

        def band(row, size):
            wide = jnp.broadcast_to(row, (size, size))
            turned = pltpu.roll(wide, 0, 1, stride=1, stride_axis=0)
            diff = lax.broadcasted_iota(jnp.int32, (size, size), 1) - lax.broadcasted_iota(jnp.int32, (size, size), 0)
            return jnp.where((diff <= 4) & (diff >= -4), turned, 0.0).astype(BF16)

        txf[i] = band(base_x[i, 1:2], 256)
        txa[i] = band(base_x[i, 0:1], 256)
        fwd = band(base_y[i, 0:1], 128)
        rows = pl.ds(pl.multiple_of(b * 128, 128), 128)
        tyf[v, rows, pl.ds(0, 128)] = fwd
        tyf[v, rows, pl.ds(128, 128)] = fwd
        tya[v, :, rows] = band(base_y[i, 1:2], 128)
        return carry

    def tiled(x, tile):
        return (x.reshape(x.shape[0] // 8, 8, 256) * tile[None]).reshape(x.shape)

    def adjoint(v, values, buf):
        def over_bases(b, carry):
            gain = scale[v * 8 + b]
            for q in range(4):
                weights = w[v, b, pl.ds(2 * q, 2)].reshape(256, 256)
                if values is not None:
                    weights = (weights.astype(F32) * values[pl.ds(2 * q, 2)].reshape(256, 256)).astype(BF16)
                o = jnp.dot(weights, txa[v * 8 + b], preferred_element_type=F32)
                for h in (0, 1):
                    z = 2 * q + h
                    if values is None:
                        tile = tiles[2] * (gain * step[0, v * 8 + z])
                    else:
                        tile = tiles[4] * gain
                    mid[z, b] = tiled(o[h * 128 : h * 128 + 128], tile).astype(BF16)
            return carry

        lax.fori_loop(0, 8, over_bases, 0)

        def over_planes(z, carry):
            o = jnp.dot(tya[v], mid[z].reshape(1024, 256), preferred_element_type=F32)
            buf[v, 4 + z] = tiled(o, tiles[3] * step[1, v * 8 + z])
            return carry

        lax.fori_loop(0, 8, over_planes, 0)

    def forward(v, last):
        def blur(z, carry):
            total = axial[v, 0] * field[z]
            for k in range(1, TAPS):
                total = total + axial[v, k] * field[z + k]
            high = total.astype(BF16)
            g[z, pl.ds(0, 128)] = high
            g[z, pl.ds(128, 128)] = (total - high.astype(F32)).astype(BF16)
            for q in range(4):
                o = jnp.dot(tyf[v, pl.ds(q * 256, 256)], g[z], preferred_element_type=F32)
                for h in (0, 1):
                    b = 2 * q + h
                    tile = tiles[0] * (scale[v * 8 + b] * step[0, v * 8 + z])
                    mid[b, z] = tiled(o[h * 128 : h * 128 + 128], tile).astype(BF16)
            return carry

        lax.fori_loop(0, 8, blur, 0)
        acc[...] = jnp.zeros_like(acc)

        def over_bases(b, carry):
            for q in range(4):
                o = jnp.dot(mid[b, pl.ds(2 * q, 2)].reshape(256, 256), txf[v * 8 + b], preferred_element_type=F32)
                acc[pl.ds(2 * q, 2)] += o.reshape(2, 128, 256) * w[v, b, pl.ds(2 * q, 2)].astype(F32)
            return carry

        lax.fori_loop(0, 8, over_bases, 0)
        if last:
            sums[v] = jnp.zeros((8, 256), F32)

        def quotient(z, carry):
            predicted = tiled(acc[z], tiles[1] * step[1, v * 8 + z])
            seen = ob[v, z]
            fraction = seen / predicted
            ratio[z] = tiled(fraction, tiles[0] * step[0, v * 8 + z])
            if last:
                terms = seen * jnp.log(fraction) - seen + predicted
                sums[v] += jnp.sum(terms.reshape(16, 8, 256), axis=0)
            return carry

        lax.fori_loop(0, 8, quotient, 0)

    def product(buf, rows, z):
        totals = []
        for v in (0, 1):
            total = axial[v, 0] * buf[v, z + 8, rows]
            for k in range(1, TAPS):
                total = total + axial[v, k] * buf[v, z + 8 - k, rows]
            totals.append(total)
        return jnp.log(totals[0] * totals[1])

    def corrections(it, c):
        rows = pl.ds(pl.multiple_of(order[c] * CHUNK, CHUNK), CHUNK)

        def each(z, carry):
            log_r[z, rows] = product(r_field, rows, z) - log_s[z, rows]
            return carry

        lax.fori_loop(0, 8, each, 0)

    def sensitivity_chunk(c):
        wait_halo_chunk(s_field, 0, c)
        rows = pl.ds(pl.multiple_of(order[c] * CHUNK, CHUNK), CHUNK)

        def each(z, carry):
            log_s[z, rows] = product(s_field, rows, z)
            return carry

        lax.fori_loop(0, 8, each, 0)

    def add_rows(start, count, ref):
        rows = pl.ds(pl.multiple_of(start, ROWS), count)
        log_r[:, rows] += ref[...]

    def reduce_chunks(it):
        hops = rs_hops(it)
        for c in range(4):
            if it == 0:
                sensitivity_chunk(c)
            wait_halo_chunk(r_field, 1 + it, c)
            corrections(it, c)
            if c == 0:
                hops[0].start()
                hops[1].start()
            if c == 1:
                hops[0].wait_recv()
                add_rows(order[1] * CHUNK, ROWS, far.at[0])
                hops[2].start()
            if c == 2:
                hops[1].wait_recv()
                add_rows(order[2] * CHUNK + ROWS, ROWS, far.at[1])
                hops[3].start()
        hops[2].wait_recv()
        add_rows(y * CHUNK, CHUNK, near.at[0])
        hops[3].wait_recv()
        add_rows(y * CHUNK, CHUNK, near.at[1])
        hops[4].start()
        hops[4].wait_recv()
        for hop in hops:
            hop.wait_send()
        wait_halo_sends(r_field, 1 + it)
        if it == 0:
            wait_halo_sends(s_field, 0)
        rows = pl.ds(pl.multiple_of(vi * ROWS, ROWS), ROWS)
        log_total = log_r[:, rows] + zbuf[...]
        return rows, field[pl.ds(4, 8), rows] * jnp.exp(log_total * (1.0 / 16.0))

    loads[0].wait()
    gather_first(0)
    lax.fori_loop(0, 16, build, 0)
    loads[1].wait()
    loads[2].wait()
    gather_second(0)
    adjoint(0, None, s_field)
    send_halos(s_field, 0, 0)
    gather_third(0)
    adjoint(1, None, s_field)
    send_halos(s_field, 0, 1)
    loads[3].wait()
    gather_last(0)
    for it in range(ITERS):
        last = it == ITERS - 1
        for v in (0, 1):
            forward(v, last)
            adjoint(v, ratio, r_field)
            send_halos(r_field, 1 + it, v)
        if last:
            for step in range(4):
                copy = remote(sums, peers.at[step], div_send.at[step], div_recv.at[step], {"depth": partners[step]})
                copy.start()
                copy.wait()
                sums[...] += peers[step]
        rows, updated = reduce_chunks(it)
        if last:
            out[...] = updated
        else:
            field[pl.ds(4, 8), rows] = updated
            gather_first(1)
            gather_second(1)
            gather_third(1)
            gather_last(1)
    for v in (0, 1):
        div_out[pl.ds(v, 1)] = jnp.broadcast_to(jnp.sum(sums[v], keepdims=True), (1, 128))


def body(estimate, observed, voxel_weights, lateral_taps, axial_taps):
    planes = observed.shape[1]
    voxel_total = planes * lax.axis_size("depth") * observed.shape[2] * observed.shape[3]
    axial = axial_taps / jnp.sum(axial_taps, axis=-1, keepdims=True)
    coarse = lax.reduce_precision(lateral_taps, 8, 7)
    totals = jnp.sum(coarse, axis=-1)
    scale = (1.0 / (totals[:, :, 0] * totals[:, :, 1])).reshape(16)
    serial = lax.axis_index("view") * 16 + jnp.arange(16)
    step = 1.0 + 0.29 * jnp.mod(0.6180339887 * serial.astype(F32) + 0.07, 1.0)
    step = jnp.stack([step, 1.0 / step])
    both = jnp.stack([coarse, coarse[..., ::-1]], axis=3).reshape(16, 2, 2, TAPS)

    def base(taps, size):
        gap = jnp.zeros((16, 2, size - TAPS), F32)
        return jnp.concatenate([taps[..., 4:], gap, taps[..., :4]], axis=-1)

    base_y = base(both[:, 0], 128)
    base_x = base(both[:, 1], 256)
    vmem = pl.BlockSpec(memory_space=pltpu.VMEM)
    smem = pl.BlockSpec(memory_space=pltpu.SMEM)
    hbm = pl.BlockSpec(memory_space=pl.ANY)
    volume = (8, 128, 256)
    updated, sums = pl.pallas_call(
        kernel,
        out_shape=(
            jax.ShapeDtypeStruct((8, ROWS, 256), F32),
            jax.ShapeDtypeStruct((2, 128), F32),
        ),
        in_specs=[hbm, hbm, hbm, vmem, vmem, smem, smem, smem, vmem],
        out_specs=(vmem, vmem),
        scratch_shapes=[
            pltpu.VMEM((2, 8) + volume, BF16),
            pltpu.VMEM((2,) + volume, F32),
            pltpu.VMEM((2, 1024, 256), BF16),
            pltpu.VMEM((2, 128, 1024), BF16),
            pltpu.VMEM((16, 256, 256), BF16),
            pltpu.VMEM((16, 256, 256), BF16),
            pltpu.VMEM((8, 256, 256), BF16),
            pltpu.VMEM((8,) + volume, BF16),
            pltpu.VMEM((16, 128, 256), F32),
            pltpu.VMEM((2, 16, 128, 256), F32),
            pltpu.VMEM((2, 16, 128, 256), F32),
            pltpu.VMEM(volume, F32),
            pltpu.VMEM(volume, F32),
            pltpu.VMEM(volume, F32),
            pltpu.VMEM(volume, F32),
            pltpu.VMEM((2, 8, ROWS, 256), F32),
            pltpu.VMEM((2, 8, CHUNK, 256), F32),
            pltpu.VMEM((8, ROWS, 256), F32),
            pltpu.VMEM((2, 8, 256), F32),
            pltpu.VMEM((4, 2, 8, 256), F32),
            pltpu.SemaphoreType.DMA((4,)),
            pltpu.SemaphoreType.DMA((2, 16)),
            pltpu.SemaphoreType.DMA((2, 16)),
            pltpu.SemaphoreType.DMA((3, 16)),
            pltpu.SemaphoreType.DMA((3, 16)),
            pltpu.SemaphoreType.DMA((2, 5)),
            pltpu.SemaphoreType.DMA((2, 5)),
            pltpu.SemaphoreType.DMA((4,)),
            pltpu.SemaphoreType.DMA((4,)),
        ],
        compiler_params=pltpu.CompilerParams(
            collective_id=0, has_side_effects=True, vmem_limit_bytes=60 * 1024 * 1024
        ),
        name="deconvolve",
    )(estimate, observed, voxel_weights, base_x, base_y, scale, axial, step, jnp.asarray(scale_tiles()))
    return updated, sums[:, 0] / voxel_total


def solution(mesh):
    placed = (
        P("depth", "view", None),
        P("view", "depth", None, None),
        P("view", None, "depth", None, None),
        P("view", None, None, None),
        P("view", None),
    )
    return jax.shard_map(
        body,
        mesh=mesh,
        in_specs=placed,
        out_specs=(P("depth", "view", None), P("view")),
        check_vma=False,
    )
```

```python
import numpy as np
import jax
import jax.numpy as jnp
from jax import lax
from jax.experimental import pallas as pl
from jax.experimental.pallas import tpu as pltpu
from jax.sharding import PartitionSpec as P

BASES = 8
TAPS = 9
RADIUS = 4
ITERS = 2
F32 = jnp.float32
BF16 = jnp.bfloat16
ROWS = 16
CHUNK = 32
HALF = 4


def spread(count, stride, reach):
    return 1.0 + reach * np.mod(stride * np.arange(count) + 0.13, 1.0)


def scale_tiles():
    rows = np.broadcast_to(spread(8, 0.5698402910, 0.37)[:, None], (8, 256))
    lanes = np.broadcast_to(spread(256, 0.7548776662, 0.41)[None, :], (8, 256))
    return np.stack([rows, 1.0 / rows, lanes, 1.0 / lanes, lanes / rows]).astype(np.float32)


def scale_steps():
    step = spread(128, 0.6180339887, 0.29)
    return np.stack([step, 1.0 / step]).astype(np.float32)


def tiled(x, tile):
    return (x.reshape(x.shape[0] // 8, 8, 256) * tile[None]).reshape(x.shape)


def kernel(
    est, obs, wgt, lateral, axial, steps, tiles,
    out, div_out,
    w, ob, tyf, tya, txf, txa, gains, coef, g, mid, mid_t, field, s_field, r_field, acc, ratio,
    log_s, log_r, far, near, zbuf, sums, peers,
    load_sem, ag_send, ag_recv, halo_send, halo_recv, rs_send, rs_recv, div_send, div_recv,
):
    vi = lax.axis_index("view")
    d = lax.axis_index("depth")
    y = vi // 2
    zl = vi % 2
    core = d % 2
    y_up = (y + 1) % 4
    y_dn = (y + 3) % 4
    v_up = y_up * 2 + zl
    v_dn = y_dn * 2 + zl
    v_z = y * 2 + 1 - zl
    v_up_z = y_up * 2 + 1 - zl
    v_dn_z = y_dn * 2 + 1 - zl
    d_up = (d + 1) % 16
    d_dn = (d + 15) % 16
    d_out = (d + 15 + 2 * core) % 16
    d_in = d + 1 - 2 * core
    partners = [d_in, d + 2 - 4 * ((d // 2) % 2), d + 4 - 8 * ((d // 4) % 2), d + 8 - 16 * (d // 8)]

    loads = [
        pltpu.make_async_copy(est, field.at[0, pl.ds(4, 8), pl.ds(pl.multiple_of(vi * ROWS, ROWS), ROWS)], load_sem.at[0]),
        pltpu.make_async_copy(wgt.at[0], w.at[0], load_sem.at[1]),
        pltpu.make_async_copy(wgt.at[1], w.at[1], load_sem.at[2]),
        pltpu.make_async_copy(obs, ob, load_sem.at[3]),
    ]
    for copy in loads:
        copy.start()

    barrier = pltpu.get_barrier_semaphore()
    greeted = [
        {"view": v_up}, {"view": v_dn}, {"view": v_z}, {"view": v_up_z}, {"view": v_dn_z},
        {"depth": d_up}, {"depth": d_dn},
        {"depth": partners[1]}, {"depth": partners[2]}, {"depth": partners[3]},
    ]
    for who in greeted:
        pl.semaphore_signal(barrier, inc=1, device_id=who, device_id_type=pl.DeviceIdType.MESH)
    pl.semaphore_wait(barrier, len(greeted))

    def remote(src, dst, send, recv, who):
        return pltpu.make_async_remote_copy(
            src_ref=src, dst_ref=dst, send_sem=send, recv_sem=recv,
            device_id=who, device_id_type=pl.DeviceIdType.MESH,
        )

    def block(it, first, count, owner):
        return field.at[it, pl.ds(first, count), pl.ds(pl.multiple_of(owner * ROWS, ROWS), ROWS)]

    hop_of = [(vi, v_z), (vi, v_up), (vi, v_dn), (vi, v_up_z), (vi, v_dn_z), (v_dn, v_up), (v_up_z, v_dn)]

    def hop(it, part, slot):
        first, count = ((4, 8), (12 * core, 4))[part]
        owner, target = hop_of[slot]
        ref = block(it, first, count, owner)
        return remote(
            ref, ref, ag_send.at[it, part * 7 + slot], ag_recv.at[it, part * 7 + slot], {"view": target}
        )

    def outer(it):
        return remote(
            block(it, 4 + 4 * core, 4, vi), block(it, 12 - 12 * core, 4, vi),
            ag_send.at[it, 14], ag_recv.at[it, 14], {"depth": d_out},
        )

    def inner(it):
        return remote(
            field.at[it, pl.ds(8 - 4 * core, 4)], field.at[it, pl.ds(12 * core, 4)],
            ag_send.at[it, 15], ag_recv.at[it, 15], {"depth": d_in},
        )

    def gather_start(it):
        outer(it).start()
        for slot in (1, 4, 0, 3, 2):
            hop(it, 0, slot).start()

    def gather_outer(it):
        outer(it).wait_recv()
        for slot in (1, 4, 0, 3, 2):
            hop(it, 1, slot).start()

    def gather_relay(it, part):
        hop(it, part, 1).wait_recv()
        hop(it, part, 5).start()
        hop(it, part, 4).wait_recv()
        hop(it, part, 6).start()

    def gather_last(it):
        for slot in (0, 2, 3, 5, 6):
            hop(it, 0, slot).wait_recv()
        inner(it).start()
        for slot in (0, 2, 3, 5, 6):
            hop(it, 1, slot).wait_recv()
        inner(it).wait_recv()
        for part in (0, 1):
            for slot in range(7):
                hop(it, part, slot).wait_send()
        outer(it).wait_send()
        inner(it).wait_send()

        @pl.when(d == 0)
        def _():
            field[it, pl.ds(0, 4)] = jnp.zeros((4, 128, 256), F32)

        @pl.when(d == 15)
        def _():
            field[it, pl.ds(12, 4)] = jnp.zeros((4, 128, 256), F32)

    order = [(y + 2) % 4, y_up, y_dn, y]

    def rows_of(c):
        return pl.ds(pl.multiple_of(order[c] * CHUNK, CHUNK), CHUNK)

    def halo(buf, turn, v, c, up):
        slot = (v * 4 + c) * 2 + up
        return remote(
            buf.at[v, pl.ds(4 + 4 * up, 4), rows_of(c)], buf.at[v, pl.ds(12 - 12 * up, 4), rows_of(c)],
            halo_send.at[turn, slot], halo_recv.at[turn, slot], {"depth": (d + 15 + 2 * up) % 16},
        )

    def wait_halo_chunk(buf, turn, c):
        for v in (0, 1):
            for up in (0, 1):
                halo(buf, turn, v, c, up).wait_recv()

        @pl.when(d == 0)
        def _():
            buf[:, pl.ds(0, 4), rows_of(c)] = jnp.zeros((2, 4, CHUNK, 256), F32)

        @pl.when(d == 15)
        def _():
            buf[:, pl.ds(12, 4), rows_of(c)] = jnp.zeros((2, 4, CHUNK, 256), F32)

    def wait_halo_sends(buf, turn):
        for v in (0, 1):
            for c in range(4):
                for up in (0, 1):
                    halo(buf, turn, v, c, up).wait_send()

    def rs_hop(it, slot):
        def cut(start, count):
            return log_r.at[:, pl.ds(pl.multiple_of(start, ROWS), count)]

        src, dst, target = [
            (cut(order[0] * CHUNK, ROWS), far.at[0], v_up),
            (cut(order[0] * CHUNK + ROWS, ROWS), far.at[1], v_dn),
            (cut(order[1] * CHUNK, CHUNK), near.at[0], v_up),
            (cut(order[2] * CHUNK, CHUNK), near.at[1], v_dn),
            (cut(v_z * ROWS, ROWS), zbuf, v_z),
        ][slot]
        return remote(src, dst, rs_send.at[it, slot], rs_recv.at[it, slot], {"view": target})

    def div_hop(step):
        return remote(sums, peers.at[step], div_send.at[step], div_recv.at[step], {"depth": partners[step]})

    def step_of(kind, v, z):
        return steps[kind, vi * 16 + v * 8 + z]

    lanes = lax.broadcasted_iota(jnp.int32, (8, 256), 1)

    def tap_row(i, axis, size, flip):
        row = jnp.zeros((8, size), F32)
        for k in range(TAPS):
            tap = lateral[i // 8, i % 8, axis, TAPS - 1 - k if flip else k]
            row = jnp.where(lanes[:, :size] == (k - RADIUS) % size, tap, row)
        return row

    def band(row, size):
        wide = jnp.broadcast_to(row[None], (size // 8, 8, size)).reshape(size, size)
        turned = pltpu.roll(wide, 0, 1, stride=1, stride_axis=0)
        diff = lax.broadcasted_iota(jnp.int32, (size, size), 1) - lax.broadcasted_iota(jnp.int32, (size, size), 0)
        return jnp.where((diff <= RADIUS) & (diff >= -RADIUS), turned, 0.0).astype(BF16)

    def build_adjoint(i, carry):
        row_x = tap_row(i, 1, 256, False)
        row_y = tap_row(i, 0, 128, True)
        txa[i] = band(row_x, 256)
        rows = pl.ds(pl.multiple_of((i % 8) * 128, 128), 128)
        tya[i // 8, :, rows] = band(row_y, 128)
        sum_x = jnp.sum(row_x.astype(BF16).astype(F32), axis=1, keepdims=True)
        sum_y = jnp.sum(row_y.astype(BF16).astype(F32), axis=1, keepdims=True)
        gains[i] = jnp.broadcast_to(1.0 / (sum_x * sum_y), (8, 256))
        return carry

    def build_forward(i, carry):
        txf[i] = band(tap_row(i, 1, 256, True), 256)
        fwd = band(tap_row(i, 0, 128, False), 128)
        rows = pl.ds(pl.multiple_of((i % 8) * 128, 128), 128)
        tyf[i // 8, rows, pl.ds(0, 128)] = fwd
        tyf[i // 8, rows, pl.ds(128, 128)] = fwd
        return carry

    def build_axial():
        for v in (0, 1):
            total = axial[v, 0]
            for k in range(1, TAPS):
                total = total + axial[v, k]
            whole = jnp.full((8, 256), total, F32)
            for k in range(TAPS):
                coef[v, k] = jnp.full((8, 256), axial[v, k], F32) / whole

    def adjoint(v, half, values, buf):
        first = 4 * half
        for b in range(BASES):
            for q in (0, 1):
                weights = w[v, b, pl.ds(first + 2 * q, 2)].reshape(256, 256)
                if values is not None:
                    weights = (weights.astype(F32) * values[pl.ds(2 * q, 2)].reshape(256, 256)).astype(BF16)
                o = jnp.dot(weights, txa[v * 8 + b], preferred_element_type=F32)
                for h in (0, 1):
                    p = 2 * q + h
                    if values is None:
                        tile = tiles[2] * gains[v * 8 + b] * step_of(0, v, first + p)
                    else:
                        tile = tiles[4] * gains[v * 8 + b]
                    mid_t[p, b] = tiled(o[h * 128 : h * 128 + 128], tile).astype(BF16)
        for p in range(HALF):
            o = jnp.dot(tya[v], mid_t[p].reshape(1024, 256), preferred_element_type=F32)
            buf[v, 4 + first + p] = tiled(o, tiles[3] * step_of(1, v, first + p))

    def forward(it, v, half):
        last = it == ITERS - 1
        first = 4 * half
        for p in range(HALF):
            z = first + p
            total = tiled(field[it, z], coef[v, 0])
            for k in range(1, TAPS):
                total = total + tiled(field[it, z + k], coef[v, k])
            high = total.astype(BF16)
            g[p, pl.ds(0, 128)] = high
            g[p, pl.ds(128, 128)] = (total - high.astype(F32)).astype(BF16)
        for p in range(HALF):
            for q in range(4):
                o = jnp.dot(tyf[v, pl.ds(q * 256, 256)], g[p], preferred_element_type=F32)
                for h in (0, 1):
                    b = 2 * q + h
                    tile = tiles[0] * gains[v * 8 + b] * step_of(0, v, first + p)
                    mid[b, p] = tiled(o[h * 128 : h * 128 + 128], tile).astype(BF16)
        for b in range(BASES):
            for q in (0, 1):
                o = jnp.dot(mid[b, pl.ds(2 * q, 2)].reshape(256, 256), txf[v * 8 + b], preferred_element_type=F32)
                o = o.reshape(2, 128, 256) * w[v, b, pl.ds(first + 2 * q, 2)].astype(F32)
                acc[pl.ds(2 * q, 2)] = o if b == 0 else acc[pl.ds(2 * q, 2)] + o
        for p in range(HALF):
            predicted = tiled(acc[p], tiles[1] * step_of(1, v, first + p))
            seen = ob[v, first + p]
            fraction = seen / predicted
            ratio[p] = tiled(fraction, tiles[0] * step_of(0, v, first + p))
            if last:
                terms = seen * jnp.log(fraction) - seen + predicted
                sums[v] += jnp.sum(terms.reshape(16, 8, 256), axis=0)

    def product(buf, rows, z):
        totals = []
        for v in (0, 1):
            total = tiled(buf[v, z + 8, rows], coef[v, 0])
            for k in range(1, TAPS):
                total = total + tiled(buf[v, z + 8 - k, rows], coef[v, k])
            totals.append(total)
        return jnp.log(totals[0] * totals[1])

    def corrections(it, c):
        rows = rows_of(c)

        def each(z, carry):
            log_r[z, rows] = product(r_field, rows, z) - log_s[z, rows]
            return carry

        lax.fori_loop(0, 8, each, 0, unroll=2)

    def sensitivity_chunk(c):
        wait_halo_chunk(s_field, 0, c)
        rows = rows_of(c)

        def each(z, carry):
            log_s[z, rows] = product(s_field, rows, z)
            return carry

        lax.fori_loop(0, 8, each, 0, unroll=2)

    def add_rows(start, count, ref):
        rows = pl.ds(pl.multiple_of(start, ROWS), count)
        log_r[:, rows] += ref[...]

    def reduce_chunks(it):
        last = it == ITERS - 1
        for c in range(4):
            if it == 0:
                sensitivity_chunk(c)
            wait_halo_chunk(r_field, 1 + it, c)
            corrections(it, c)
            if c == 0:
                rs_hop(it, 0).start()
                rs_hop(it, 1).start()
            if c == 1:
                rs_hop(it, 0).wait_recv()
                add_rows(order[1] * CHUNK, ROWS, far.at[0])
                rs_hop(it, 2).start()
            if c == 2:
                rs_hop(it, 1).wait_recv()
                add_rows(order[2] * CHUNK + ROWS, ROWS, far.at[1])
                rs_hop(it, 3).start()
            if last:
                div_hop(c).wait()
                sums[...] += peers[c]
                if c < 3:
                    div_hop(c + 1).start()
        rs_hop(it, 2).wait_recv()
        add_rows(y * CHUNK, CHUNK, near.at[0])
        rs_hop(it, 3).wait_recv()
        add_rows(y * CHUNK, CHUNK, near.at[1])
        rs_hop(it, 4).start()
        rs_hop(it, 4).wait_recv()
        rows = pl.ds(pl.multiple_of(vi * ROWS, ROWS), ROWS)
        log_total = log_r[:, rows] + zbuf[...]
        return rows, field[it, pl.ds(4, 8), rows] * jnp.exp(log_total * (1.0 / 16.0))

    def drain(it):
        for slot in range(5):
            rs_hop(it, slot).wait_send()
        wait_halo_sends(r_field, 1 + it)
        if it == 0:
            wait_halo_sends(s_field, 0)

    def sensitivity(v):
        def each(s, carry):
            half = (s + core) % 2
            adjoint(v, half, None, s_field)
            for c in range(4):
                halo(s_field, 0, v, c, half).start()
            return carry

        lax.fori_loop(0, 2, each, 0)

    def project(it):
        last = it == ITERS - 1
        if last:
            sums[...] = jnp.zeros((2, 8, 256), F32)

        def each(s, carry):
            v = s // 2
            half = (s + core) % 2
            forward(it, v, half)
            adjoint(v, half, ratio, r_field)
            for c in range(4):
                halo(r_field, 1 + it, v, c, half).start()
            return carry

        lax.fori_loop(0, 4, each, 0)

    loads[0].wait()
    gather_start(0)
    lax.fori_loop(0, 8, build_adjoint, 0)
    loads[1].wait()
    sensitivity(0)
    gather_outer(0)
    gather_relay(0, 0)
    lax.fori_loop(8, 16, build_adjoint, 0)
    loads[2].wait()
    sensitivity(1)
    gather_relay(0, 1)
    build_axial()
    lax.fori_loop(0, 16, build_forward, 0)
    loads[3].wait()
    gather_last(0)
    for it in range(ITERS):
        last = it == ITERS - 1
        project(it)
        if last:
            div_hop(0).start()
        rows, updated = reduce_chunks(it)
        if last:
            out[...] = updated
        else:
            field[1, pl.ds(4, 8), rows] = updated
            gather_start(1)
            gather_outer(1)
            gather_relay(1, 0)
            gather_relay(1, 1)
        drain(it)
        if not last:
            gather_last(1)
    for v in (0, 1):
        div_out[v] = jnp.sum(sums[v]) * (1.0 / (128 * 128 * 256))


def body(estimate, observed, voxel_weights, lateral_taps, axial_taps):
    vmem = pl.BlockSpec(memory_space=pltpu.VMEM)
    smem = pl.BlockSpec(memory_space=pltpu.SMEM)
    hbm = pl.BlockSpec(memory_space=pl.ANY)
    volume = (8, 128, 256)
    part = (HALF, 128, 256)
    return pl.pallas_call(
        kernel,
        out_shape=(
            jax.ShapeDtypeStruct((8, ROWS, 256), F32),
            jax.ShapeDtypeStruct((2,), F32),
        ),
        in_specs=[hbm, hbm, hbm, smem, smem, smem, vmem],
        out_specs=(vmem, smem),
        scratch_shapes=[
            pltpu.VMEM((2, 8) + volume, BF16),
            pltpu.VMEM((2,) + volume, F32),
            pltpu.VMEM((2, 1024, 256), BF16),
            pltpu.VMEM((2, 128, 1024), BF16),
            pltpu.VMEM((16, 256, 256), BF16),
            pltpu.VMEM((16, 256, 256), BF16),
            pltpu.VMEM((16, 8, 256), F32),
            pltpu.VMEM((2, TAPS, 8, 256), F32),
            pltpu.VMEM((HALF, 256, 256), BF16),
            pltpu.VMEM((8,) + part, BF16),
            pltpu.VMEM((HALF, 8, 128, 256), BF16),
            pltpu.VMEM((2, 16, 128, 256), F32),
            pltpu.VMEM((2, 16, 128, 256), F32),
            pltpu.VMEM((2, 16, 128, 256), F32),
            pltpu.VMEM(part, F32),
            pltpu.VMEM(part, F32),
            pltpu.VMEM(volume, F32),
            pltpu.VMEM(volume, F32),
            pltpu.VMEM((2, 8, ROWS, 256), F32),
            pltpu.VMEM((2, 8, CHUNK, 256), F32),
            pltpu.VMEM((8, ROWS, 256), F32),
            pltpu.VMEM((2, 8, 256), F32),
            pltpu.VMEM((4, 2, 8, 256), F32),
            pltpu.SemaphoreType.DMA((4,)),
            pltpu.SemaphoreType.DMA((2, 16)),
            pltpu.SemaphoreType.DMA((2, 16)),
            pltpu.SemaphoreType.DMA((3, 16)),
            pltpu.SemaphoreType.DMA((3, 16)),
            pltpu.SemaphoreType.DMA((2, 5)),
            pltpu.SemaphoreType.DMA((2, 5)),
            pltpu.SemaphoreType.DMA((4,)),
            pltpu.SemaphoreType.DMA((4,)),
        ],
        compiler_params=pltpu.CompilerParams(
            collective_id=0, has_side_effects=True, vmem_limit_bytes=60 * 1024 * 1024
        ),
        name="deconvolve",
    )(
        estimate, observed, voxel_weights, lateral_taps, axial_taps,
        jnp.asarray(scale_steps()), jnp.asarray(scale_tiles()),
    )


def solution(mesh):
    placed = (
        P("depth", "view", None),
        P("view", "depth", None, None),
        P("view", None, "depth", None, None),
        P("view", None, None, None),
        P("view", None),
    )
    return jax.shard_map(
        body,
        mesh=mesh,
        in_specs=placed,
        out_specs=(P("depth", "view", None), P("view")),
        check_vma=False,
    )
```

```python
import numpy as np
import jax
import jax.numpy as jnp
from jax import lax
from jax.experimental import pallas as pl
from jax.experimental.pallas import tpu as pltpu
from jax.sharding import PartitionSpec as P

BASES = 8
TAPS = 9
RADIUS = 4
ITERS = 2
F32 = jnp.float32
BF16 = jnp.bfloat16
ROWS = 16
CHUNK = 32
HALF = 4


def spread(count, stride, reach):
    return 1.0 + reach * np.mod(stride * np.arange(count) + 0.13, 1.0)


def scale_tiles():
    rows = np.broadcast_to(spread(8, 0.5698402910, 0.37)[:, None], (8, 256))
    lanes = np.broadcast_to(spread(256, 0.7548776662, 0.41)[None, :], (8, 256))
    return np.stack([rows, 1.0 / rows, lanes, 1.0 / lanes, lanes / rows]).astype(np.float32)


def scale_steps():
    step = spread(128, 0.6180339887, 0.29)
    return np.stack([step, 1.0 / step]).astype(np.float32)


def tiled(x, tile):
    return (x.reshape(x.shape[0] // 8, 8, 256) * tile[None]).reshape(x.shape)


def kernel(
    est, obs, wgt, lateral, axial, steps, tiles,
    out, div_out,
    w, ob, tyf, tya, txf, txa, gains, coef, g, mid, mid_t, field, s_field, r_field, acc, ratio,
    log_s, log_r, far, near, zbuf, sums, peers,
    load_sem, ag_send, ag_recv, halo_send, halo_recv, rs_send, rs_recv, div_send, div_recv,
):
    vi = lax.axis_index("view")
    d = lax.axis_index("depth")
    y = vi // 2
    zl = vi % 2
    core = d % 2
    y_up = (y + 1) % 4
    y_dn = (y + 3) % 4
    v_up = y_up * 2 + zl
    v_dn = y_dn * 2 + zl
    v_z = y * 2 + 1 - zl
    v_up_z = y_up * 2 + 1 - zl
    v_dn_z = y_dn * 2 + 1 - zl
    d_up = (d + 1) % 16
    d_dn = (d + 15) % 16
    d_out = (d + 15 + 2 * core) % 16
    d_in = d + 1 - 2 * core
    partners = [d_in, d + 2 - 4 * ((d // 2) % 2), d + 4 - 8 * ((d // 4) % 2), d + 8 - 16 * (d // 8)]

    loads = [
        pltpu.make_async_copy(est, field.at[0, pl.ds(4, 8), pl.ds(pl.multiple_of(vi * ROWS, ROWS), ROWS)], load_sem.at[0]),
        pltpu.make_async_copy(wgt.at[0], w.at[0], load_sem.at[1]),
        pltpu.make_async_copy(wgt.at[1], w.at[1], load_sem.at[2]),
        pltpu.make_async_copy(obs, ob, load_sem.at[3]),
    ]
    loads[0].start()
    loads[1].start()

    barrier = pltpu.get_barrier_semaphore()
    greeted = [
        {"view": v_up}, {"view": v_dn}, {"view": v_z}, {"view": v_up_z}, {"view": v_dn_z},
        {"depth": d_up}, {"depth": d_dn},
        {"depth": partners[1]}, {"depth": partners[2]}, {"depth": partners[3]},
    ]
    for who in greeted:
        pl.semaphore_signal(barrier, inc=1, device_id=who, device_id_type=pl.DeviceIdType.MESH)
    pl.semaphore_wait(barrier, len(greeted))

    def remote(src, dst, send, recv, who):
        return pltpu.make_async_remote_copy(
            src_ref=src, dst_ref=dst, send_sem=send, recv_sem=recv,
            device_id=who, device_id_type=pl.DeviceIdType.MESH,
        )

    def block(it, first, count, owner):
        return field.at[it, pl.ds(first, count), pl.ds(pl.multiple_of(owner * ROWS, ROWS), ROWS)]

    straight = [(vi, v_z), (vi, v_up), (vi, v_dn), (v_z, v_up), (v_z, v_dn), (v_dn, v_up), (v_up_z, v_dn)]
    diagonal = straight[:3] + [(vi, v_up_z), (vi, v_dn_z)] + straight[5:]

    inner_plane = 4 - 4 * core
    outer_plane = 4 * core
    plane_of = [inner_plane, outer_plane]

    def hop(it, part, slot):
        first = (4 + inner_plane, 4 + outer_plane, 12 * core)[part]
        owner, target = (diagonal if it == 1 and part > 0 else straight)[slot]
        ref = block(it, first, 4, owner)
        return remote(
            ref, ref, ag_send.at[it, part * 7 + slot], ag_recv.at[it, part * 7 + slot], {"view": target}
        )

    def outer(it):
        return remote(
            block(it, 4 + 4 * core, 4, vi), block(it, 12 - 12 * core, 4, vi),
            ag_send.at[it, 21], ag_recv.at[it, 21], {"depth": d_out},
        )

    def inner(it):
        return remote(
            field.at[it, pl.ds(8 - 4 * core, 4)], field.at[it, pl.ds(12 * core, 4)],
            ag_send.at[it, 22], ag_recv.at[it, 22], {"depth": d_in},
        )

    def gather_own(it, part):
        for slot in (1, 4, 0, 3, 2) if it == 1 and part > 0 else (0, 1, 2):
            hop(it, part, slot).start()

    def gather_near(it, part):
        if not (it == 1 and part > 0):
            hop(it, part, 0).wait_recv()
            hop(it, part, 4).start()
            hop(it, part, 3).start()
        hop(it, part, 1).wait_recv()
        hop(it, part, 5).start()

    def gather_far(it, part):
        hop(it, part, 4).wait_recv()
        hop(it, part, 6).start()

    def gather_rest(it, part):
        for slot in (0, 2, 3, 5, 6) if it == 1 and part > 0 else (2, 3, 5, 6):
            hop(it, part, slot).wait_recv()

    def gather_last(it):
        for part in (1, 2):
            gather_rest(it, part)
        inner(it).wait_recv()
        for part in (0, 1, 2):
            for slot in range(7):
                hop(it, part, slot).wait_send()
        outer(it).wait_send()
        inner(it).wait_send()

        @pl.when(d == 0)
        def _():
            field[it, pl.ds(0, 4)] = jnp.zeros((4, 128, 256), F32)

        @pl.when(d == 15)
        def _():
            field[it, pl.ds(12, 4)] = jnp.zeros((4, 128, 256), F32)

    order = [(y + 2) % 4, y_up, y_dn, y]

    def rows_of(c):
        return pl.ds(pl.multiple_of(order[c] * CHUNK, CHUNK), CHUNK)

    def halo(buf, turn, v, c, up):
        slot = (v * 4 + c) * 2 + up
        return remote(
            buf.at[v, pl.ds(4 + 4 * up, 4), rows_of(c)], buf.at[v, pl.ds(12 - 12 * up, 4), rows_of(c)],
            halo_send.at[turn, slot], halo_recv.at[turn, slot], {"depth": (d + 15 + 2 * up) % 16},
        )

    def wait_halo_chunk(buf, turn, phase, c):
        up = (core, 1 - core)[phase]
        for v in (0, 1):
            halo(buf, turn, v, c, up).wait_recv()
        if phase == 1:

            @pl.when(d == 0)
            def _():
                buf[:, pl.ds(0, 4), rows_of(c)] = jnp.zeros((2, 4, CHUNK, 256), F32)

            @pl.when(d == 15)
            def _():
                buf[:, pl.ds(12, 4), rows_of(c)] = jnp.zeros((2, 4, CHUNK, 256), F32)

    def wait_halo_sends(buf, turn):
        for v in (0, 1):
            for c in range(4):
                for up in (0, 1):
                    halo(buf, turn, v, c, up).wait_send()

    def rs_hop(it, phase, slot):
        def cut(start, count):
            return log_r.at[pl.ds(plane_of[phase], 4), pl.ds(pl.multiple_of(start, ROWS), count)]

        src, dst, target = [
            (cut(order[0] * CHUNK, ROWS), far.at[phase, 0], v_up),
            (cut(order[0] * CHUNK + ROWS, ROWS), far.at[phase, 1], v_dn),
            (cut(order[1] * CHUNK, CHUNK), near.at[phase, 0], v_up),
            (cut(order[2] * CHUNK, CHUNK), near.at[phase, 1], v_dn),
            (cut(v_z * ROWS, ROWS), zbuf.at[phase], v_z),
        ][slot]
        return remote(
            src, dst, rs_send.at[it, phase * 5 + slot], rs_recv.at[it, phase * 5 + slot], {"view": target}
        )

    def div_hop(step):
        return remote(sums, peers.at[step], div_send.at[step], div_recv.at[step], {"depth": partners[step]})

    def step_of(kind, v, z):
        return steps[kind, vi * 16 + v * 8 + z]

    lanes = lax.broadcasted_iota(jnp.int32, (8, 256), 1)

    def tap_row(i, axis, size, flip):
        row = jnp.zeros((8, size), F32)
        for k in range(TAPS):
            tap = lateral[i // 8, i % 8, axis, TAPS - 1 - k if flip else k]
            row = jnp.where(lanes[:, :size] == (k - RADIUS) % size, tap, row)
        return row

    def band(row, size):
        wide = jnp.broadcast_to(row[None], (size // 8, 8, size)).reshape(size, size)
        turned = pltpu.roll(wide, 0, 1, stride=1, stride_axis=0)
        diff = lax.broadcasted_iota(jnp.int32, (size, size), 1) - lax.broadcasted_iota(jnp.int32, (size, size), 0)
        return jnp.where((diff <= RADIUS) & (diff >= -RADIUS), turned, 0.0).astype(BF16)

    def build_adjoint(i, carry):
        row_x = tap_row(i, 1, 256, False)
        row_y = tap_row(i, 0, 128, True)
        txa[i] = band(row_x, 256)
        rows = pl.ds(pl.multiple_of((i % 8) * 128, 128), 128)
        tya[i // 8, :, rows] = band(row_y, 128)
        sum_x = jnp.sum(row_x.astype(BF16).astype(F32), axis=1, keepdims=True)
        sum_y = jnp.sum(row_y.astype(BF16).astype(F32), axis=1, keepdims=True)
        gains[i] = jnp.broadcast_to(1.0 / (sum_x * sum_y), (8, 256))
        return carry

    def build_forward(i, carry):
        txf[i] = band(tap_row(i, 1, 256, True), 256)
        fwd = band(tap_row(i, 0, 128, False), 128)
        rows = pl.ds(pl.multiple_of((i % 8) * 128, 128), 128)
        tyf[i // 8, rows, pl.ds(0, 128)] = fwd
        tyf[i // 8, rows, pl.ds(128, 128)] = fwd
        return carry

    def build_axial():
        for v in (0, 1):
            total = axial[v, 0]
            for k in range(1, TAPS):
                total = total + axial[v, k]
            whole = jnp.full((8, 256), total, F32)
            for k in range(TAPS):
                coef[v, k] = jnp.full((8, 256), axial[v, k], F32) / whole

    def adjoint(v, half, values, buf):
        first = 4 * half
        for b in range(BASES):
            for q in (0, 1):
                weights = w[v, b, pl.ds(first + 2 * q, 2)].reshape(256, 256)
                if values is not None:
                    weights = (weights.astype(F32) * values[pl.ds(2 * q, 2)].reshape(256, 256)).astype(BF16)
                o = jnp.dot(weights, txa[v * 8 + b], preferred_element_type=F32)
                for h in (0, 1):
                    p = 2 * q + h
                    if values is None:
                        tile = tiles[2] * gains[v * 8 + b] * step_of(0, v, first + p)
                    else:
                        tile = tiles[4] * gains[v * 8 + b]
                    mid_t[p, b] = tiled(o[h * 128 : h * 128 + 128], tile).astype(BF16)
        for p in range(HALF):
            o = jnp.dot(tya[v], mid_t[p].reshape(1024, 256), preferred_element_type=F32)
            buf[v, 4 + first + p] = tiled(o, tiles[3] * step_of(1, v, first + p))

    def forward(it, v, half):
        last = it == ITERS - 1
        first = 4 * half
        for p in range(HALF):
            z = first + p
            total = tiled(field[it, z], coef[v, 0])
            for k in range(1, TAPS):
                total = total + tiled(field[it, z + k], coef[v, k])
            high = total.astype(BF16)
            g[p, pl.ds(0, 128)] = high
            g[p, pl.ds(128, 128)] = (total - high.astype(F32)).astype(BF16)
        for p in range(HALF):
            for q in range(4):
                o = jnp.dot(tyf[v, pl.ds(q * 256, 256)], g[p], preferred_element_type=F32)
                for h in (0, 1):
                    b = 2 * q + h
                    tile = tiles[0] * gains[v * 8 + b] * step_of(0, v, first + p)
                    mid[b, p] = tiled(o[h * 128 : h * 128 + 128], tile).astype(BF16)
        for b in range(BASES):
            for q in (0, 1):
                o = jnp.dot(mid[b, pl.ds(2 * q, 2)].reshape(256, 256), txf[v * 8 + b], preferred_element_type=F32)
                o = o.reshape(2, 128, 256) * w[v, b, pl.ds(first + 2 * q, 2)].astype(F32)
                acc[pl.ds(2 * q, 2)] = o if b == 0 else acc[pl.ds(2 * q, 2)] + o
        for p in range(HALF):
            predicted = tiled(acc[p], tiles[1] * step_of(1, v, first + p))
            seen = ob[v, first + p]
            fraction = seen / predicted
            ratio[p] = tiled(fraction, tiles[0] * step_of(0, v, first + p))
            if last:
                terms = seen * jnp.log(fraction) - seen + predicted
                sums[v] += jnp.sum(terms.reshape(16, 8, 256), axis=0)

    def product(buf, rows, z):
        totals = []
        for v in (0, 1):
            total = tiled(buf[v, z + 8, rows], coef[v, 0])
            for k in range(1, TAPS):
                total = total + tiled(buf[v, z + 8 - k, rows], coef[v, k])
            totals.append(total)
        return jnp.log(totals[0] * totals[1])

    def corrections(it, phase, c):
        rows = rows_of(c)

        def each(j, carry):
            z = plane_of[phase] + j
            log_r[z, rows] = product(r_field, rows, z) - log_s[z, rows]
            return carry

        lax.fori_loop(0, 4, each, 0, unroll=2)

    def sensitivity_chunk(phase, c):
        rows = rows_of(c)

        def each(j, carry):
            z = plane_of[phase] + j
            log_s[z, rows] = product(s_field, rows, z)
            return carry

        lax.fori_loop(0, 4, each, 0, unroll=2)

    def add_rows(phase, start, count, ref):
        rows = pl.ds(pl.multiple_of(start, ROWS), count)
        log_r[pl.ds(plane_of[phase], 4), rows] += ref[...]

    def reduce_phase(it, phase, between):
        for c in range(4):
            if it == 0:
                wait_halo_chunk(s_field, 0, phase, c)
                sensitivity_chunk(phase, c)
            wait_halo_chunk(r_field, 1 + it, phase, c)
            corrections(it, phase, c)
            if c == 0:
                rs_hop(it, phase, 0).start()
                rs_hop(it, phase, 1).start()
            if c == 1:
                rs_hop(it, phase, 0).wait_recv()
                add_rows(phase, order[1] * CHUNK, ROWS, far.at[phase, 0])
                rs_hop(it, phase, 2).start()
            if c == 2:
                rs_hop(it, phase, 1).wait_recv()
                add_rows(phase, order[2] * CHUNK + ROWS, ROWS, far.at[phase, 1])
                rs_hop(it, phase, 3).start()
            between(c)
        rs_hop(it, phase, 2).wait_recv()
        add_rows(phase, y * CHUNK, CHUNK, near.at[phase, 0])
        rs_hop(it, phase, 3).wait_recv()
        add_rows(phase, y * CHUNK, CHUNK, near.at[phase, 1])
        rs_hop(it, phase, 4).start()

    def finish(it, phase):
        rs_hop(it, phase, 4).wait_recv()
        rows = pl.ds(pl.multiple_of(vi * ROWS, ROWS), ROWS)
        log_total = log_r[pl.ds(plane_of[phase], 4), rows] + zbuf[phase]
        updated = field[it, pl.ds(4 + plane_of[phase], 4), rows] * jnp.exp(log_total * (1.0 / 16.0))
        if it == ITERS - 1:
            out[pl.ds(plane_of[phase], 4)] = updated
        else:
            field[it + 1, pl.ds(4 + plane_of[phase], 4), rows] = updated

    def outer_between(it):
        def run(c):
            if it == 0:
                if c == 1:
                    finish(0, 0)
                    gather_own(1, 0)
                if c == 3:
                    gather_near(1, 0)
            elif c == 0:
                div_hop(0).start()
            else:
                div_hop(c - 1).wait()
                sums[...] += peers[c - 1]
                div_hop(c).start()

        return run

    def drain(it):
        for phase in (0, 1):
            for slot in range(5):
                rs_hop(it, phase, slot).wait_send()
        wait_halo_sends(r_field, 1 + it)
        if it == 0:
            wait_halo_sends(s_field, 0)

    def sensitivity(v, half):
        adjoint(v, half, None, s_field)

    def send_sensitivity(v, half):
        for c in range(4):
            halo(s_field, 0, v, c, half).start()

    def project(it):
        last = it == ITERS - 1
        if last:
            sums[...] = jnp.zeros((2, 8, 256), F32)

        def each(s, carry):
            v = s // 2
            half = (s + core) % 2
            forward(it, v, half)
            adjoint(v, half, ratio, r_field)
            for c in range(4):
                halo(r_field, 1 + it, v, c, half).start()
            return carry

        lax.fori_loop(0, 4, each, 0)

    loads[0].wait()
    outer(0).start()
    gather_own(0, 1)
    gather_own(0, 0)
    lax.fori_loop(0, 8, build_adjoint, 0)
    loads[1].wait()
    loads[2].start()
    loads[3].start()
    sensitivity(0, core)
    outer(0).wait_recv()
    gather_own(0, 2)
    send_sensitivity(0, core)
    sensitivity(0, 1 - core)
    send_sensitivity(0, 1 - core)
    gather_near(0, 1)
    gather_near(0, 0)
    lax.fori_loop(8, 16, build_adjoint, 0)
    loads[2].wait()

    def each_half(s, carry):
        half = (s + core) % 2
        sensitivity(1, half)
        send_sensitivity(1, half)
        return carry

    lax.fori_loop(0, 2, each_half, 0)
    gather_far(0, 1)
    gather_far(0, 0)
    gather_near(0, 2)
    build_axial()
    lax.fori_loop(0, 16, build_forward, 0)
    loads[3].wait()
    gather_far(0, 2)
    gather_rest(0, 0)
    inner(0).start()
    gather_last(0)
    for it in range(ITERS):
        project(it)
        reduce_phase(it, 0, lambda c: None)
        reduce_phase(it, 1, outer_between(it))
        if it == 0:
            gather_far(1, 0)
            finish(0, 1)
            outer(1).start()
            gather_own(1, 1)
            gather_rest(1, 0)
            inner(1).start()
            outer(1).wait_recv()
            gather_own(1, 2)
            for part in (1, 2):
                gather_near(1, part)
                gather_far(1, part)
        else:
            finish(1, 0)
            div_hop(3).wait()
            sums[...] += peers[3]
            finish(1, 1)
        drain(it)
        if it == 0:
            gather_last(1)
    for v in (0, 1):
        div_out[v] = jnp.sum(sums[v]) * (1.0 / (128 * 128 * 256))


def body(estimate, observed, voxel_weights, lateral_taps, axial_taps):
    vmem = pl.BlockSpec(memory_space=pltpu.VMEM)
    smem = pl.BlockSpec(memory_space=pltpu.SMEM)
    hbm = pl.BlockSpec(memory_space=pl.ANY)
    volume = (8, 128, 256)
    part = (HALF, 128, 256)
    return pl.pallas_call(
        kernel,
        out_shape=(
            jax.ShapeDtypeStruct((8, ROWS, 256), F32),
            jax.ShapeDtypeStruct((2,), F32),
        ),
        in_specs=[hbm, hbm, hbm, smem, smem, smem, vmem],
        out_specs=(vmem, smem),
        scratch_shapes=[
            pltpu.VMEM((2, 8) + volume, BF16),
            pltpu.VMEM((2,) + volume, F32),
            pltpu.VMEM((2, 1024, 256), BF16),
            pltpu.VMEM((2, 128, 1024), BF16),
            pltpu.VMEM((16, 256, 256), BF16),
            pltpu.VMEM((16, 256, 256), BF16),
            pltpu.VMEM((16, 8, 256), F32),
            pltpu.VMEM((2, TAPS, 8, 256), F32),
            pltpu.VMEM((HALF, 256, 256), BF16),
            pltpu.VMEM((8,) + part, BF16),
            pltpu.VMEM((HALF, 8, 128, 256), BF16),
            pltpu.VMEM((2, 16, 128, 256), F32),
            pltpu.VMEM((2, 16, 128, 256), F32),
            pltpu.VMEM((2, 16, 128, 256), F32),
            pltpu.VMEM(part, F32),
            pltpu.VMEM(part, F32),
            pltpu.VMEM(volume, F32),
            pltpu.VMEM(volume, F32),
            pltpu.VMEM((2, 2, 4, ROWS, 256), F32),
            pltpu.VMEM((2, 2, 4, CHUNK, 256), F32),
            pltpu.VMEM((2, 4, ROWS, 256), F32),
            pltpu.VMEM((2, 8, 256), F32),
            pltpu.VMEM((4, 2, 8, 256), F32),
            pltpu.SemaphoreType.DMA((4,)),
            pltpu.SemaphoreType.DMA((2, 23)),
            pltpu.SemaphoreType.DMA((2, 23)),
            pltpu.SemaphoreType.DMA((3, 16)),
            pltpu.SemaphoreType.DMA((3, 16)),
            pltpu.SemaphoreType.DMA((2, 10)),
            pltpu.SemaphoreType.DMA((2, 10)),
            pltpu.SemaphoreType.DMA((4,)),
            pltpu.SemaphoreType.DMA((4,)),
        ],
        compiler_params=pltpu.CompilerParams(
            collective_id=0, has_side_effects=True, vmem_limit_bytes=60 * 1024 * 1024
        ),
        name="deconvolve",
    )(
        estimate, observed, voxel_weights, lateral_taps, axial_taps,
        jnp.asarray(scale_steps()), jnp.asarray(scale_tiles()),
    )


def solution(mesh):
    placed = (
        P("depth", "view", None),
        P("view", "depth", None, None),
        P("view", None, "depth", None, None),
        P("view", None, None, None),
        P("view", None),
    )
    return jax.shard_map(
        body,
        mesh=mesh,
        in_specs=placed,
        out_specs=(P("depth", "view", None), P("view")),
        check_vma=False,
    )
```

```python
import numpy as np
import jax
import jax.numpy as jnp
from jax import lax
from jax.experimental import pallas as pl
from jax.experimental.pallas import tpu as pltpu
from jax.sharding import PartitionSpec as P

BASES = 8
TAPS = 9
RADIUS = 4
ITERS = 2
F32 = jnp.float32
BF16 = jnp.bfloat16
ROWS = 16
CHUNK = 32
HALF = 4


def spread(count, stride, reach):
    return 1.0 + reach * np.mod(stride * np.arange(count) + 0.13, 1.0)


def scale_tiles():
    rows = np.broadcast_to(spread(8, 0.5698402910, 0.37)[:, None], (8, 256))
    lanes = np.broadcast_to(spread(256, 0.7548776662, 0.41)[None, :], (8, 256))
    return np.stack([rows, 1.0 / rows, lanes, 1.0 / lanes, lanes / rows]).astype(np.float32)


def scale_steps():
    step = spread(128, 0.6180339887, 0.29)
    return np.stack([step, 1.0 / step]).astype(np.float32)


def tiled(x, tile):
    return (x.reshape(x.shape[0] // 8, 8, 256) * tile[None]).reshape(x.shape)


def kernel(
    est, obs, wgt, lateral, axial, steps, tiles,
    out, div_out,
    w, ob, tyf, tya, txf, txa, gains, coef, g, mid, mid_t, field, s_field, r_field, acc, ratio,
    log_s, log_r, far, near, zbuf, sums, peers,
    load_sem, ag_send, ag_recv, halo_send, halo_recv, rs_send, rs_recv, div_send, div_recv,
):
    vi = lax.axis_index("view")
    d = lax.axis_index("depth")
    y = vi // 2
    zl = vi % 2
    core = d % 2
    y_up = (y + 1) % 4
    y_dn = (y + 3) % 4
    v_up = y_up * 2 + zl
    v_dn = y_dn * 2 + zl
    v_z = y * 2 + 1 - zl
    v_up_z = y_up * 2 + 1 - zl
    v_dn_z = y_dn * 2 + 1 - zl
    d_up = (d + 1) % 16
    d_dn = (d + 15) % 16
    d_out = (d + 15 + 2 * core) % 16
    d_in = d + 1 - 2 * core
    partners = [d_in, d + 2 - 4 * ((d // 2) % 2), d + 4 - 8 * ((d // 4) % 2), d + 8 - 16 * (d // 8)]

    loads = [
        pltpu.make_async_copy(est, field.at[0, pl.ds(4, 8), pl.ds(pl.multiple_of(vi * ROWS, ROWS), ROWS)], load_sem.at[0]),
        pltpu.make_async_copy(wgt.at[0, :, pl.ds(4 * core, 4)], w.at[0, :, pl.ds(4 * core, 4)], load_sem.at[1]),
        pltpu.make_async_copy(wgt.at[1], w.at[1], load_sem.at[2]),
        pltpu.make_async_copy(obs, ob, load_sem.at[3]),
        pltpu.make_async_copy(wgt.at[0, :, pl.ds(4 - 4 * core, 4)], w.at[0, :, pl.ds(4 - 4 * core, 4)], load_sem.at[4]),
    ]
    for which in (0, 1, 4):
        loads[which].start()

    barrier = pltpu.get_barrier_semaphore()
    greeted = [
        {"view": v_up}, {"view": v_dn}, {"view": v_z}, {"view": v_up_z}, {"view": v_dn_z},
        {"depth": d_up}, {"depth": d_dn},
        {"depth": partners[1]}, {"depth": partners[2]}, {"depth": partners[3]},
    ]
    for who in greeted:
        pl.semaphore_signal(barrier, inc=1, device_id=who, device_id_type=pl.DeviceIdType.MESH)

    def remote(src, dst, send, recv, who):
        return pltpu.make_async_remote_copy(
            src_ref=src, dst_ref=dst, send_sem=send, recv_sem=recv,
            device_id=who, device_id_type=pl.DeviceIdType.MESH,
        )

    def block(it, first, count, owner):
        return field.at[it, pl.ds(first, count), pl.ds(pl.multiple_of(owner * ROWS, ROWS), ROWS)]

    straight = [(vi, v_z), (vi, v_up), (vi, v_dn), (v_z, v_up), (v_z, v_dn), (v_dn, v_up), (v_up_z, v_dn)]
    diagonal = straight[:3] + [(vi, v_up_z), (vi, v_dn_z)] + straight[5:]

    inner_plane = 4 - 4 * core
    outer_plane = 4 * core
    plane_of = [inner_plane, outer_plane]

    def hop(it, part, slot):
        first = (4 + inner_plane, 4 + outer_plane, 12 * core)[part]
        owner, target = (diagonal if it == 1 and part > 0 else straight)[slot]
        ref = block(it, first, 4, owner)
        return remote(
            ref, ref, ag_send.at[it, part * 7 + slot], ag_recv.at[it, part * 7 + slot], {"view": target}
        )

    def outer(it):
        return remote(
            block(it, 4 + 4 * core, 4, vi), block(it, 12 - 12 * core, 4, vi),
            ag_send.at[it, 21], ag_recv.at[it, 21], {"depth": d_out},
        )

    def inner(it):
        return remote(
            field.at[it, pl.ds(8 - 4 * core, 4)], field.at[it, pl.ds(12 * core, 4)],
            ag_send.at[it, 22], ag_recv.at[it, 22], {"depth": d_in},
        )

    def gather_own(it, part):
        for slot in (1, 4, 0, 3, 2) if it == 1 and part > 0 else (0, 1, 2):
            hop(it, part, slot).start()

    def gather_near(it, part):
        if not (it == 1 and part > 0):
            hop(it, part, 0).wait_recv()
            hop(it, part, 4).start()
            hop(it, part, 3).start()
        hop(it, part, 1).wait_recv()
        hop(it, part, 5).start()

    def gather_far(it, part):
        hop(it, part, 4).wait_recv()
        hop(it, part, 6).start()

    def gather_rest(it, part):
        for slot in (0, 2, 3, 5, 6) if it == 1 and part > 0 else (2, 3, 5, 6):
            hop(it, part, slot).wait_recv()

    def gather_last(it):
        for part in (1, 2):
            gather_rest(it, part)
        inner(it).wait_recv()
        for part in (0, 1, 2):
            for slot in range(7):
                hop(it, part, slot).wait_send()
        outer(it).wait_send()
        inner(it).wait_send()

        @pl.when(d == 0)
        def _():
            field[it, pl.ds(0, 4)] = jnp.zeros((4, 128, 256), F32)

        @pl.when(d == 15)
        def _():
            field[it, pl.ds(12, 4)] = jnp.zeros((4, 128, 256), F32)

    order = [(y + 2) % 4, y_up, y_dn, y]

    def rows_of(c):
        return pl.ds(pl.multiple_of(order[c] * CHUNK, CHUNK), CHUNK)

    def halo(buf, turn, v, c, up):
        slot = (v * 4 + c) * 2 + up
        return remote(
            buf.at[v, pl.ds(4 + 4 * up, 4), rows_of(c)], buf.at[v, pl.ds(12 - 12 * up, 4), rows_of(c)],
            halo_send.at[turn, slot], halo_recv.at[turn, slot], {"depth": (d + 15 + 2 * up) % 16},
        )

    def wait_halo_chunk(buf, turn, phase, c):
        up = (core, 1 - core)[phase]
        for v in (0, 1):
            halo(buf, turn, v, c, up).wait_recv()
        if phase == 1:

            @pl.when(d == 0)
            def _():
                buf[:, pl.ds(0, 4), rows_of(c)] = jnp.zeros((2, 4, CHUNK, 256), F32)

            @pl.when(d == 15)
            def _():
                buf[:, pl.ds(12, 4), rows_of(c)] = jnp.zeros((2, 4, CHUNK, 256), F32)

    def wait_halo_sends(buf, turn):
        for v in (0, 1):
            for c in range(4):
                for up in (0, 1):
                    halo(buf, turn, v, c, up).wait_send()

    def rs_hop(it, phase, slot):
        def cut(start, count):
            return log_r.at[pl.ds(plane_of[phase], 4), pl.ds(pl.multiple_of(start, ROWS), count)]

        src, dst, target = [
            (cut(order[0] * CHUNK, ROWS), far.at[phase, 0], v_up),
            (cut(order[0] * CHUNK + ROWS, ROWS), far.at[phase, 1], v_dn),
            (cut(order[1] * CHUNK, CHUNK), near.at[phase, 0], v_up),
            (cut(order[2] * CHUNK, CHUNK), near.at[phase, 1], v_dn),
            (cut(v_z * ROWS, ROWS), zbuf.at[phase], v_z),
        ][slot]
        return remote(
            src, dst, rs_send.at[it, phase * 5 + slot], rs_recv.at[it, phase * 5 + slot], {"view": target}
        )

    def div_hop(step):
        return remote(sums, peers.at[step], div_send.at[step], div_recv.at[step], {"depth": partners[step]})

    def step_of(kind, v, z):
        return steps[kind, vi * 16 + v * 8 + z]

    lanes = lax.broadcasted_iota(jnp.int32, (8, 256), 1)

    def tap_row(i, axis, size, flip):
        row = jnp.zeros((8, size), F32)
        for k in range(TAPS):
            tap = lateral[i // 8, i % 8, axis, TAPS - 1 - k if flip else k]
            row = jnp.where(lanes[:, :size] == (k - RADIUS) % size, tap, row)
        return row

    def band(row, size):
        wide = jnp.broadcast_to(row[None], (size // 8, 8, size)).reshape(size, size)
        turned = pltpu.roll(wide, 0, 1, stride=1, stride_axis=0)
        diff = lax.broadcasted_iota(jnp.int32, (size, size), 1) - lax.broadcasted_iota(jnp.int32, (size, size), 0)
        return jnp.where((diff <= RADIUS) & (diff >= -RADIUS), turned, 0.0).astype(BF16)

    def build_adjoint(i, carry):
        row_x = tap_row(i, 1, 256, False)
        row_y = tap_row(i, 0, 128, True)
        txa[i] = band(row_x, 256)
        rows = pl.ds(pl.multiple_of((i % 8) * 128, 128), 128)
        tya[i // 8, :, rows] = band(row_y, 128)
        sum_x = jnp.sum(row_x.astype(BF16).astype(F32), axis=1, keepdims=True)
        sum_y = jnp.sum(row_y.astype(BF16).astype(F32), axis=1, keepdims=True)
        gains[i] = jnp.broadcast_to(1.0 / (sum_x * sum_y), (8, 256))
        return carry

    def build_forward(i, carry):
        txf[i] = band(tap_row(i, 1, 256, True), 256)
        fwd = band(tap_row(i, 0, 128, False), 128)
        rows = pl.ds(pl.multiple_of((i % 8) * 128, 128), 128)
        tyf[i // 8, rows, pl.ds(0, 128)] = fwd
        tyf[i // 8, rows, pl.ds(128, 128)] = fwd
        return carry

    def build_axial():
        for v in (0, 1):
            total = axial[v, 0]
            for k in range(1, TAPS):
                total = total + axial[v, k]
            whole = jnp.full((8, 256), total, F32)
            for k in range(TAPS):
                coef[v, k] = jnp.full((8, 256), axial[v, k], F32) / whole

    def adjoint(v, half, values, buf):
        first = 4 * half
        for b in range(BASES):
            for q in (0, 1):
                weights = w[v, b, pl.ds(first + 2 * q, 2)].reshape(256, 256)
                if values is not None:
                    weights = (weights.astype(F32) * values[pl.ds(2 * q, 2)].reshape(256, 256)).astype(BF16)
                o = jnp.dot(weights, txa[v * 8 + b], preferred_element_type=F32)
                for h in (0, 1):
                    p = 2 * q + h
                    if values is None:
                        tile = tiles[2] * gains[v * 8 + b] * step_of(0, v, first + p)
                    else:
                        tile = tiles[4] * gains[v * 8 + b]
                    mid_t[p, b] = tiled(o[h * 128 : h * 128 + 128], tile).astype(BF16)
        for p in range(HALF):
            o = jnp.dot(tya[v], mid_t[p].reshape(1024, 256), preferred_element_type=F32)
            buf[v, 4 + first + p] = tiled(o, tiles[3] * step_of(1, v, first + p))

    def forward(it, v, half):
        last = it == ITERS - 1
        first = 4 * half
        for p in range(HALF):
            z = first + p
            total = tiled(field[it, z], coef[v, 0])
            for k in range(1, TAPS):
                total = total + tiled(field[it, z + k], coef[v, k])
            high = total.astype(BF16)
            g[p, pl.ds(0, 128)] = high
            g[p, pl.ds(128, 128)] = (total - high.astype(F32)).astype(BF16)
        for p in range(HALF):
            for q in range(4):
                o = jnp.dot(tyf[v, pl.ds(q * 256, 256)], g[p], preferred_element_type=F32)
                for h in (0, 1):
                    b = 2 * q + h
                    tile = tiles[0] * gains[v * 8 + b] * step_of(0, v, first + p)
                    mid[b, p] = tiled(o[h * 128 : h * 128 + 128], tile).astype(BF16)
        for b in range(BASES):
            for q in (0, 1):
                o = jnp.dot(mid[b, pl.ds(2 * q, 2)].reshape(256, 256), txf[v * 8 + b], preferred_element_type=F32)
                o = o.reshape(2, 128, 256) * w[v, b, pl.ds(first + 2 * q, 2)].astype(F32)
                acc[pl.ds(2 * q, 2)] = o if b == 0 else acc[pl.ds(2 * q, 2)] + o
        for p in range(HALF):
            predicted = tiled(acc[p], tiles[1] * step_of(1, v, first + p))
            seen = ob[v, first + p]
            fraction = seen / predicted
            ratio[p] = tiled(fraction, tiles[0] * step_of(0, v, first + p))
            if last:
                terms = seen * jnp.log(fraction) - seen + predicted
                sums[v] += jnp.sum(terms.reshape(16, 8, 256), axis=0)

    def product(buf, rows, z):
        totals = []
        for v in (0, 1):
            total = tiled(buf[v, z + 8, rows], coef[v, 0])
            for k in range(1, TAPS):
                total = total + tiled(buf[v, z + 8 - k, rows], coef[v, k])
            totals.append(total)
        return jnp.log(totals[0] * totals[1])

    def corrections(it, phase, c):
        rows = rows_of(c)

        def each(j, carry):
            z = plane_of[phase] + j
            log_r[z, rows] = product(r_field, rows, z) - log_s[z, rows]
            return carry

        lax.fori_loop(0, 4, each, 0, unroll=2)

    def sensitivity_chunk(phase, c):
        rows = rows_of(c)

        def each(j, carry):
            z = plane_of[phase] + j
            log_s[z, rows] = product(s_field, rows, z)
            return carry

        lax.fori_loop(0, 4, each, 0, unroll=2)

    def add_rows(phase, start, count, ref):
        rows = pl.ds(pl.multiple_of(start, ROWS), count)
        log_r[pl.ds(plane_of[phase], 4), rows] += ref[...]

    def reduce_phase(it, phase, between):
        for c in range(4):
            if it == 0:
                wait_halo_chunk(s_field, 0, phase, c)
                sensitivity_chunk(phase, c)
            wait_halo_chunk(r_field, 1 + it, phase, c)
            corrections(it, phase, c)
            if c == 0:
                rs_hop(it, phase, 0).start()
                rs_hop(it, phase, 1).start()
            if c == 1:
                rs_hop(it, phase, 0).wait_recv()
                add_rows(phase, order[1] * CHUNK, ROWS, far.at[phase, 0])
                rs_hop(it, phase, 2).start()
            if c == 2:
                rs_hop(it, phase, 1).wait_recv()
                add_rows(phase, order[2] * CHUNK + ROWS, ROWS, far.at[phase, 1])
                rs_hop(it, phase, 3).start()
            between(c)
        rs_hop(it, phase, 2).wait_recv()
        add_rows(phase, y * CHUNK, CHUNK, near.at[phase, 0])
        rs_hop(it, phase, 3).wait_recv()
        add_rows(phase, y * CHUNK, CHUNK, near.at[phase, 1])
        rs_hop(it, phase, 4).start()

    def finish(it, phase):
        rs_hop(it, phase, 4).wait_recv()
        rows = pl.ds(pl.multiple_of(vi * ROWS, ROWS), ROWS)
        log_total = log_r[pl.ds(plane_of[phase], 4), rows] + zbuf[phase]
        updated = field[it, pl.ds(4 + plane_of[phase], 4), rows] * jnp.exp(log_total * (1.0 / 16.0))
        if it == ITERS - 1:
            out[pl.ds(plane_of[phase], 4)] = updated
        else:
            field[it + 1, pl.ds(4 + plane_of[phase], 4), rows] = updated

    def outer_between(it):
        def run(c):
            if it == 0:
                if c == 1:
                    finish(0, 0)
                    gather_own(1, 0)
                if c == 3:
                    gather_near(1, 0)
            elif c == 0:
                div_hop(0).start()
            else:
                div_hop(c - 1).wait()
                sums[...] += peers[c - 1]
                div_hop(c).start()

        return run

    def drain(it):
        for phase in (0, 1):
            for slot in range(5):
                rs_hop(it, phase, slot).wait_send()
        wait_halo_sends(r_field, 1 + it)
        if it == 0:
            wait_halo_sends(s_field, 0)

    def sensitivity(v, half):
        adjoint(v, half, None, s_field)

    def send_sensitivity(v, half):
        for c in range(4):
            halo(s_field, 0, v, c, half).start()

    def project(it):
        last = it == ITERS - 1
        if last:
            sums[...] = jnp.zeros((2, 8, 256), F32)

        def each(s, carry):
            v = s // 2
            half = (s + core) % 2
            forward(it, v, half)
            adjoint(v, half, ratio, r_field)
            for c in range(4):
                halo(r_field, 1 + it, v, c, half).start()
            return carry

        lax.fori_loop(0, 4, each, 0)

    lax.fori_loop(0, 8, build_adjoint, 0)
    loads[0].wait()
    pl.semaphore_wait(barrier, len(greeted))
    outer(0).start()
    gather_own(0, 1)
    gather_own(0, 0)
    loads[1].wait()
    loads[2].start()
    loads[3].start()
    sensitivity(0, core)
    outer(0).wait_recv()
    gather_own(0, 2)
    send_sensitivity(0, core)
    loads[4].wait()
    sensitivity(0, 1 - core)
    send_sensitivity(0, 1 - core)
    gather_near(0, 1)
    gather_near(0, 0)
    lax.fori_loop(8, 16, build_adjoint, 0)
    loads[2].wait()

    def each_half(s, carry):
        half = (s + core) % 2
        sensitivity(1, half)
        send_sensitivity(1, half)
        return carry

    lax.fori_loop(0, 2, each_half, 0)
    gather_far(0, 1)
    gather_far(0, 0)
    gather_near(0, 2)
    build_axial()
    lax.fori_loop(0, 16, build_forward, 0)
    loads[3].wait()
    gather_far(0, 2)
    gather_rest(0, 0)
    inner(0).start()
    gather_last(0)
    for it in range(ITERS):
        project(it)
        reduce_phase(it, 0, lambda c: None)
        reduce_phase(it, 1, outer_between(it))
        if it == 0:
            gather_far(1, 0)
            finish(0, 1)
            outer(1).start()
            gather_own(1, 1)
            gather_rest(1, 0)
            inner(1).start()
            outer(1).wait_recv()
            gather_own(1, 2)
            for part in (1, 2):
                gather_near(1, part)
                gather_far(1, part)
        else:
            finish(1, 0)
            div_hop(3).wait()
            sums[...] += peers[3]
            finish(1, 1)
        drain(it)
        if it == 0:
            gather_last(1)
    for v in (0, 1):
        div_out[v] = jnp.sum(sums[v]) * (1.0 / (128 * 128 * 256))


def body(estimate, observed, voxel_weights, lateral_taps, axial_taps):
    vmem = pl.BlockSpec(memory_space=pltpu.VMEM)
    smem = pl.BlockSpec(memory_space=pltpu.SMEM)
    hbm = pl.BlockSpec(memory_space=pl.ANY)
    volume = (8, 128, 256)
    part = (HALF, 128, 256)
    return pl.pallas_call(
        kernel,
        out_shape=(
            jax.ShapeDtypeStruct((8, ROWS, 256), F32),
            jax.ShapeDtypeStruct((2,), F32),
        ),
        in_specs=[hbm, hbm, hbm, smem, smem, smem, vmem],
        out_specs=(vmem, smem),
        scratch_shapes=[
            pltpu.VMEM((2, 8) + volume, BF16),
            pltpu.VMEM((2,) + volume, F32),
            pltpu.VMEM((2, 1024, 256), BF16),
            pltpu.VMEM((2, 128, 1024), BF16),
            pltpu.VMEM((16, 256, 256), BF16),
            pltpu.VMEM((16, 256, 256), BF16),
            pltpu.VMEM((16, 8, 256), F32),
            pltpu.VMEM((2, TAPS, 8, 256), F32),
            pltpu.VMEM((HALF, 256, 256), BF16),
            pltpu.VMEM((8,) + part, BF16),
            pltpu.VMEM((HALF, 8, 128, 256), BF16),
            pltpu.VMEM((2, 16, 128, 256), F32),
            pltpu.VMEM((2, 16, 128, 256), F32),
            pltpu.VMEM((2, 16, 128, 256), F32),
            pltpu.VMEM(part, F32),
            pltpu.VMEM(part, F32),
            pltpu.VMEM(volume, F32),
            pltpu.VMEM(volume, F32),
            pltpu.VMEM((2, 2, 4, ROWS, 256), F32),
            pltpu.VMEM((2, 2, 4, CHUNK, 256), F32),
            pltpu.VMEM((2, 4, ROWS, 256), F32),
            pltpu.VMEM((2, 8, 256), F32),
            pltpu.VMEM((4, 2, 8, 256), F32),
            pltpu.SemaphoreType.DMA((5,)),
            pltpu.SemaphoreType.DMA((2, 23)),
            pltpu.SemaphoreType.DMA((2, 23)),
            pltpu.SemaphoreType.DMA((3, 16)),
            pltpu.SemaphoreType.DMA((3, 16)),
            pltpu.SemaphoreType.DMA((2, 10)),
            pltpu.SemaphoreType.DMA((2, 10)),
            pltpu.SemaphoreType.DMA((4,)),
            pltpu.SemaphoreType.DMA((4,)),
        ],
        compiler_params=pltpu.CompilerParams(
            collective_id=0, has_side_effects=True, vmem_limit_bytes=60 * 1024 * 1024
        ),
        name="deconvolve",
    )(
        estimate, observed, voxel_weights, lateral_taps, axial_taps,
        jnp.asarray(scale_steps()), jnp.asarray(scale_tiles()),
    )


def solution(mesh):
    placed = (
        P("depth", "view", None),
        P("view", "depth", None, None),
        P("view", None, "depth", None, None),
        P("view", None, None, None),
        P("view", None),
    )
    return jax.shard_map(
        body,
        mesh=mesh,
        in_specs=placed,
        out_specs=(P("depth", "view", None), P("view")),
        check_vma=False,
    )
```
